32 devices in a mesh: band: 8 (over z, y), grid: 4 (over x, core).
Axes of the slice: x: 2, y: 2, z: 4, core: 2. Of those that a mesh axis runs over, the one named last changes fastest.
Arguments:
- bands: bfloat16 [2, 16, 128, 128, 128], P(None, 'band', 'grid'), may hold values from -6 to 6
- occupations: float32 [16], P('band'), may hold values from 0.25 to 1
- external: float32 [128, 128, 128], P('grid'), may hold values from 0 to 2
- density_in: float32 [128, 128, 128], P('grid'), may hold values from -0.2 to 1.4
- prev_density: float32 [128, 128, 128], P('grid'), may hold values from 0 to 1.2
- prev_residual: float32 [128, 128, 128], P('grid'), may hold values from -1.3 to 0.3
- hist_density: float32 [5, 128, 128, 128], P(None, 'grid'), may hold values from 0 to 1
- hist_residual: float32 [5, 128, 128, 128], P(None, 'grid'), may hold values from -0.6 to 1
Outputs:
- density: float32 [128, 128, 128], P('grid')
- residual: float32 [128, 128, 128], P('grid')
The draws below stay inside these ranges and needn't reach their ends.
All inputs are finite; a program needn't handle non-finite values.
Results may differ from the reference program's by a relative error of at most 0.018.
The reference program's roundings to bfloat16 on the way count: a program that leaves them out, or rounds other values in their place, can miss the bound.
Values may be sent and summed in bfloat16 or wider, within the bound.
A program may use at most 192 MiB of HBM per device.

```python
import math
import jax
import jax.numpy as jnp
from jax import lax

NG = 128
DEPTH = 6
ITERS = 3
BANDS = 16


def draw_density_in(key, part):
    jitter = jax.random.uniform(key, (NG, NG, NG), jnp.float32, -0.4, 0.4)
    position = jnp.arange(NG, dtype=jnp.float32)[:, None, None] / (NG - 1)
    return 0.2 + 0.8 * position + jitter


def draw_prev_residual(key, part):
    jitter = jax.random.uniform(jax.random.fold_in(key, 11), (NG, NG, NG), jnp.float32, -0.3, 0.3)
    position = jnp.arange(NG, dtype=jnp.float32)[:, None, None] / (NG - 1)
    return -(0.2 + 0.8 * position) + jitter


def draw_hist_residual(key, part):
    jitter = jax.random.uniform(jax.random.fold_in(key, 23), (DEPTH - 1, NG, NG, NG), jnp.float32, -0.3, 0.3)
    position = jnp.arange(NG, dtype=jnp.float32) / (NG - 1)
    order = DEPTH - 1 - jnp.arange(DEPTH - 1, dtype=jnp.float32)
    profile = 0.2 + 0.5 * jnp.cos(math.pi * order[:, None] * position[None, :])
    return profile[:, :, None, None] + jitter


def level_of(rng, shape, cuts, least, largest):
    level = 1.0
    for axis_at, parts in cuts:
        draws = jax.random.uniform(jax.random.fold_in(jax.random.fold_in(rng, 6), axis_at), (parts,), jnp.float32, least / len(cuts), largest / len(cuts))
        level = level * jnp.repeat(jnp.exp(draws), shape[axis_at] // parts).reshape((-1,) + (1,) * (len(shape) - 1 - axis_at))
    return level


def scatter_about(key, shape, spread, reach, shards=(), held_as=jnp.bfloat16):
    entries = jax.random.normal(key, shape, jnp.float32) * spread
    if len(shards) > 0:
        entries = level_of(key, shape, shards, -0.22, 0.18) * entries
    return jnp.clip(entries, min=-reach, max=reach).astype(held_as)


def setup_inputs(seed: int = 0) -> dict:
    streams_of = jax.random.split(jax.random.key(seed), 9)
    bands = scatter_about(streams_of[0], (2, BANDS, NG, NG, NG), 1.0, 6.0, ((1, 8), (2, 4)))
    occupations = jnp.clip(jnp.exp(math.log(1.0) - 1.3862944 * jax.random.uniform(streams_of[1], (BANDS,), jnp.float32) ** level_of(streams_of[1], (BANDS,), ((0, 8),), -0.2, 0.2)), 0.25, 1.0)
    external = jnp.clip(2.0 * jax.random.uniform(streams_of[2], (NG, NG, NG), jnp.float32) ** level_of(streams_of[2], (NG, NG, NG), ((0, 4),), -0.2, 0.2), 0.0, 2.0)
    density_in = draw_density_in(jax.random.fold_in(streams_of[8], 71), 0)
    prev_density = jnp.clip(1.2 * jax.random.uniform(streams_of[4], (NG, NG, NG), jnp.float32) ** level_of(streams_of[4], (NG, NG, NG), ((0, 4),), -0.2, 0.2), 0.0, 1.2)
    prev_residual = draw_prev_residual(jax.random.fold_in(streams_of[8], 71), 0)
    hist_density = jnp.clip(1.0 * jax.random.uniform(streams_of[6], (DEPTH - 1, NG, NG, NG), jnp.float32) ** level_of(streams_of[6], (DEPTH - 1, NG, NG, NG), ((1, 4),), -0.2, 0.2), 0.0, 1.0)
    hist_residual = draw_hist_residual(jax.random.fold_in(streams_of[8], 71), 0)
    return dict(bands=bands, occupations=occupations, external=external, density_in=density_in, prev_density=prev_density, prev_residual=prev_residual, hist_density=hist_density, hist_residual=hist_residual)


time_step = 0.25
energy_shift = 2.5
coupling = 1.0
mixing_weight = 0.5
ridge_share = 0.1
ridge_floor = 0.01
density_scale = 8.0
highest = lax.Precision.HIGHEST

def fourier_tables(length, frequency):
    positions = jnp.arange(length, dtype=jnp.int32)
    phase_index = positions[:, None] * frequency[None, :] % length
    angles = phase_index.astype(jnp.float32) * (2.0 * math.pi / length)
    unit_scale = 1.0 / math.sqrt(length)
    return ((jnp.cos(angles) * unit_scale).astype(jnp.bfloat16), (jnp.sin(angles) * unit_scale).astype(jnp.bfloat16))

def solve_definite(matrix, vector):
    extent = matrix.shape[0]
    factor_low = jnp.zeros_like(matrix)
    for column in range(extent):
        pivot_value = jnp.sqrt(matrix[column, column] - jnp.sum(factor_low[column, :column] * factor_low[column, :column]))
        factor_low = factor_low.at[column, column].set(pivot_value)
        for row_index in range(column + 1, extent):
            element = (matrix[row_index, column] - jnp.sum(factor_low[row_index, :column] * factor_low[column, :column])) / pivot_value
            factor_low = factor_low.at[row_index, column].set(element)
    middle = jnp.zeros_like(vector)
    for row_index in range(extent):
        element = (vector[row_index] - jnp.sum(factor_low[row_index, :row_index] * middle[:row_index])) / factor_low[row_index, row_index]
        middle = middle.at[row_index].set(element)
    result = jnp.zeros_like(vector)
    for row_index in reversed(range(extent)):
        element = (middle[row_index] - jnp.sum(factor_low[row_index + 1:, row_index] * result[row_index + 1:])) / factor_low[row_index, row_index]
        result = result.at[row_index].set(element)
    return result

def contract(operand, matrix):
    return jnp.einsum('abl,lk->abk', operand, matrix, precision=highest)

def along_axis(real_part, imag_part, cosine_part, sine_part, orientation, axis_index):
    cosine_wide = cosine_part.astype(jnp.float32)
    sine_wide = sine_part.astype(jnp.float32) * orientation
    real_moved = jnp.moveaxis(real_part.astype(jnp.float32), axis_index, -1)
    imag_moved = jnp.moveaxis(imag_part.astype(jnp.float32), axis_index, -1)
    out_real = contract(real_moved, cosine_wide) - contract(imag_moved, sine_wide)
    out_imag = contract(real_moved, sine_wide) + contract(imag_moved, cosine_wide)
    return (jnp.moveaxis(out_real, -1, axis_index), jnp.moveaxis(out_imag, -1, axis_index))

def band_step(real_part, imag_part, factor, kinetic, tables):
    cosine_part, sine_part = tables
    real_part = (real_part.astype(jnp.float32) * factor).astype(jnp.bfloat16)
    imag_part = (imag_part.astype(jnp.float32) * factor).astype(jnp.bfloat16)
    for axis_index in (2, 1):
        real_part, imag_part = along_axis(real_part, imag_part, cosine_part, sine_part, -1.0, axis_index)
        real_part = real_part.astype(jnp.bfloat16)
        imag_part = imag_part.astype(jnp.bfloat16)
    real_part, imag_part = along_axis(real_part, imag_part, cosine_part, sine_part, -1.0, 0)
    real_part = (real_part * kinetic).astype(jnp.bfloat16)
    imag_part = (imag_part * kinetic).astype(jnp.bfloat16)
    for axis_index in (0, 1, 2):
        real_part, imag_part = along_axis(real_part, imag_part, cosine_part.T, sine_part.T, 1.0, axis_index)
        real_part = real_part.astype(jnp.bfloat16)
        imag_part = imag_part.astype(jnp.bfloat16)
    return (real_part, imag_part)

def reference(bands, occupations, external, density_in, prev_density, prev_residual, hist_density, hist_residual):
    frequency = jnp.arange(-(NG // 4), NG // 4, dtype=jnp.int32)
    tables = fourier_tables(NG, frequency)
    squared = frequency.astype(jnp.float32) * frequency.astype(jnp.float32)
    quarter = NG / 4.0
    radius = squared[:, None, None] + squared[None, :, None] + squared[None, None, :]
    kinetic = jnp.exp(-time_step * radius / (quarter * quarter))
    cells_total = NG * NG * NG
    real_bands = bands[0]
    imag_bands = bands[1]
    density_now = density_in
    density_prev = prev_density
    residual_prev = prev_residual
    density_diffs = hist_density
    residual_diffs = hist_residual
    residual = density_in
    for iteration in range(ITERS):
        factor = jnp.exp(-time_step * (external + coupling * density_now - energy_shift))

        def one_band(accumulated, slices):
            real_part, imag_part, weight = slices
            real_part, imag_part = band_step(real_part, imag_part, factor, kinetic, tables)
            wide_real = real_part.astype(jnp.float32)
            wide_imag = imag_part.astype(jnp.float32)
            return (accumulated + weight * (wide_real * wide_real + wide_imag * wide_imag), (real_part, imag_part))
        accumulated, (real_bands, imag_bands) = lax.scan(one_band, jnp.zeros((NG, NG, NG), jnp.float32), (real_bands, imag_bands, occupations))
        density_out = accumulated * (density_scale / BANDS)
        residual = density_out - density_now
        density_diffs = jnp.concatenate([density_diffs[density_diffs.shape[0] - (DEPTH - 1):], (density_now - density_prev)[None]], axis=0)
        residual_diffs = jnp.concatenate([residual_diffs[residual_diffs.shape[0] - (DEPTH - 1):], (residual - residual_prev)[None]], axis=0)
        flat_diffs = residual_diffs.reshape(DEPTH, -1)
        gram_matrix = jnp.dot(flat_diffs, flat_diffs.T, precision=highest) / cells_total
        right_side = jnp.dot(flat_diffs, residual.reshape(-1), precision=highest) / cells_total
        ridge_value = ridge_share * jnp.trace(gram_matrix) / DEPTH + ridge_floor
        coeffs = solve_definite(gram_matrix + ridge_value * jnp.eye(DEPTH, dtype=jnp.float32), right_side)
        combined = density_diffs + mixing_weight * residual_diffs
        density_next = density_now + mixing_weight * residual - jnp.einsum('j,jxyz->xyz', coeffs, combined, precision=highest)
        density_prev = density_now
        residual_prev = residual
        density_now = density_next
    return (density_now, residual)
```

```python
import math

import jax
import jax.numpy as jnp
from jax import lax
from jax.experimental import pallas as pl
from jax.experimental.pallas import tpu as pltpu
from jax.sharding import PartitionSpec as P

NG = 128
DEPTH = 6
ITERS = 3


time_step = 0.25
energy_shift = 2.5
coupling = 1.0
mixing_weight = 0.5
ridge_share = 0.1
ridge_floor = 0.01
density_scale = 8.0
highest = lax.Precision.HIGHEST


def fourier_tables(length, frequency):
    positions = jnp.arange(length, dtype=jnp.int32)
    phase_index = positions[:, None] * frequency[None, :] % length
    angles = phase_index.astype(jnp.float32) * (2.0 * math.pi / length)
    unit_scale = 1.0 / math.sqrt(length)
    return (
        (jnp.cos(angles) * unit_scale).astype(jnp.bfloat16),
        (jnp.sin(angles) * unit_scale).astype(jnp.bfloat16),
    )


def complex_block(cosine_part, sine_part, orientation):
    sine_signed = sine_part * orientation
    upper_half = jnp.concatenate([cosine_part, sine_signed], axis=1)
    lower_half = jnp.concatenate([-sine_signed, cosine_part], axis=1)
    return jnp.concatenate([upper_half, lower_half], axis=0)


def fold(cells):
    return jnp.sum(cells.reshape(-1, 8, cells.shape[-1]), axis=0)


def gram_kernel(hist_ref, out_ref):
    @pl.when(pl.program_id(0) == 0)
    def _():
        out_ref[...] = jnp.zeros_like(out_ref)

    count = hist_ref.shape[0]
    for plane in range(hist_ref.shape[1]):
        entries = [hist_ref[j, plane] for j in range(count)]
        place = 0
        for j in range(count):
            for k in range(j + 1):
                out_ref[place] += fold(entries[j] * entries[k])
                place += 1


def kept_products(hist):
    count, planes, rows, lanes = hist.shape
    pairs = count * (count + 1) // 2
    return pl.pallas_call(
        gram_kernel,
        grid=(planes // 2,),
        in_specs=[pl.BlockSpec((count, 2, rows, lanes), lambda i: (0, i, 0, 0))],
        out_specs=pl.BlockSpec((pairs, 8, lanes), lambda i: (0, 0, 0)),
        out_shape=jax.ShapeDtypeStruct((pairs, 8, lanes), jnp.float32),
        compiler_params=pltpu.CompilerParams(dimension_semantics=("arbitrary",)),
    )(hist)


def sums_kernel(first, fresh_count, *refs):
    hist_ref = refs[0]
    fresh = refs[1 : 1 + fresh_count]
    total_ref, now_ref, before_ref, residual_ref, newest_ref, out_ref = refs[1 + fresh_count :]

    @pl.when(pl.program_id(0) == 0)
    def _():
        out_ref[...] = jnp.zeros_like(out_ref)

    for plane in range(hist_ref.shape[1]):
        residual = total_ref[plane].astype(jnp.float32) - now_ref[plane]
        newest = residual - before_ref[plane]
        residual_ref[plane] = residual
        newest_ref[plane] = newest
        entries = [hist_ref[j, plane] for j in range(first, hist_ref.shape[0])]
        entries += [ref[plane] for ref in fresh] + [newest]
        for j, entry in enumerate(entries):
            out_ref[j] += fold(entry * newest)
            out_ref[len(entries) + j] += fold(entry * residual)


def residual_sums(first, hist, fresh, total, now, before):
    count, planes, rows, lanes = hist.shape
    cell = pl.BlockSpec((2, rows, lanes), lambda i: (i, 0, 0))
    field = jax.ShapeDtypeStruct((planes, rows, lanes), jnp.float32)
    entries = count - first + len(fresh) + 1
    return pl.pallas_call(
        lambda *refs: sums_kernel(first, len(fresh), *refs),
        grid=(planes // 2,),
        in_specs=[pl.BlockSpec((count, 2, rows, lanes), lambda i: (0, i, 0, 0))]
        + [cell] * (len(fresh) + 3),
        out_specs=(cell, cell, pl.BlockSpec((2 * entries, 8, lanes), lambda i: (0, 0, 0))),
        out_shape=(field, field, jax.ShapeDtypeStruct((2 * entries, 8, lanes), jnp.float32)),
        compiler_params=pltpu.CompilerParams(dimension_semantics=("arbitrary",)),
    )(hist, *fresh, total, now, before)


def solve_kernel(kept_ref, sums_ref, coeffs_ref, next_ref):
    last = DEPTH - 1
    shape = (8, coeffs_ref.shape[1])

    def spot(j, k):
        return j * (j + 1) // 2 + k

    values = {}
    for j in range(DEPTH):
        for k in range(j + 1):
            values[j, k] = sums_ref[k] if j == last else kept_ref[spot(j, k)]
    for j in range(last):
        for k in range(j + 1):
            next_ref[spot(j, k)] = values[j + 1, k + 1]
    trace = values[0, 0]
    for j in range(1, DEPTH):
        trace = trace + values[j, j]
    ridge = trace * (ridge_share / DEPTH) + ridge_floor
    matrix = {}
    for (j, k), value in values.items():
        matrix[j, k] = jnp.full(shape, value + ridge if j == k else value, jnp.float32)
    vector = [jnp.full(shape, sums_ref[DEPTH + j], jnp.float32) for j in range(DEPTH)]
    inverse = []
    for k in range(DEPTH):
        inverse.append(1.0 / matrix[k, k])
        scaled = {j: matrix[j, k] * inverse[k] for j in range(k + 1, DEPTH)}
        for j in range(k + 1, DEPTH):
            vector[j] = vector[j] - scaled[j] * vector[k]
            for m in range(k + 1, j + 1):
                matrix[j, m] = matrix[j, m] - scaled[j] * matrix[m, k]
    for k in reversed(range(DEPTH)):
        value = vector[k]
        for j in range(k + 1, DEPTH):
            value = value - matrix[j, k] * vector[j]
        vector[k] = value * inverse[k]
    for k in range(DEPTH):
        coeffs_ref[pl.ds(k, 1), :] = vector[k][:1]


def solve_definite(kept, sums, lanes):
    scalars = pl.BlockSpec(memory_space=pltpu.SMEM)
    return pl.pallas_call(
        solve_kernel,
        in_specs=[scalars, scalars],
        out_specs=(pl.BlockSpec(memory_space=pltpu.VMEM), scalars),
        out_shape=(
            jax.ShapeDtypeStruct((DEPTH, lanes), jnp.float32),
            jax.ShapeDtypeStruct(kept.shape, jnp.float32),
        ),
    )(kept, sums)


def local(
    bands,
    occupations,
    external,
    density_in,
    prev_density,
    prev_residual,
    hist_density,
    hist_residual,
):
    grid_count = lax.axis_size("grid")
    band_count = lax.axis_size("band")
    slab_planes = external.shape[0]
    cells_total = NG * NG * NG
    bands_total = occupations.shape[0] * band_count
    frequency = jnp.arange(-(NG // 4), NG // 4, dtype=jnp.int32)
    kept_count = frequency.shape[0]
    inside = ((frequency >= -(NG // 4)) & (frequency < NG // 4)).astype(jnp.float32)
    cosine_part, sine_part = fourier_tables(NG, frequency)
    forward_block = complex_block(cosine_part, sine_part, -1.0)
    inverse_block = complex_block(cosine_part.T, sine_part.T, 1.0)
    forward_axis = forward_block.reshape(2, NG, 2, kept_count)
    inverse_axis = inverse_block.reshape(2, kept_count, 2, NG)
    column_rows = kept_count // grid_count
    column_start = lax.axis_index("grid") * column_rows
    local_freq = lax.dynamic_slice_in_dim(frequency, column_start, column_rows).astype(jnp.float32)
    local_inside = lax.dynamic_slice_in_dim(inside, column_start, column_rows)
    squared = frequency.astype(jnp.float32) * frequency.astype(jnp.float32)
    quarter = NG / 4.0
    radius = (
        squared[None, :, None] + (local_freq * local_freq)[:, None, None] + squared[None, None, :]
    )
    kinetic = jnp.exp(-time_step * radius / (quarter * quarter))
    kinetic = kinetic * local_inside[:, None, None] * inside[None, :, None] * inside[None, None, :]
    gram_kept = lax.psum(
        jnp.sum(kept_products(hist_residual), axis=(1, 2)) / cells_total, "grid"
    )
    orbitals = jnp.concatenate([bands[0], bands[1]], axis=-1)
    density_now = density_in
    density_prev = prev_density
    residual_prev = prev_residual
    density_diffs = [hist_density[j] for j in range(DEPTH - 1)]
    residual_diffs = [hist_residual[j] for j in range(DEPTH - 1)]
    fresh = []
    residual = density_in
    for iteration in range(ITERS):
        factor = jnp.exp(-time_step * (external + coupling * density_now - energy_shift))
        doubled = jnp.concatenate([factor, factor], axis=-1)
        weighted = (orbitals.astype(jnp.float32) * doubled).astype(jnp.bfloat16)
        band_items = orbitals.shape[0]
        along_z = jnp.dot(weighted, forward_block, preferred_element_type=jnp.float32).astype(
            jnp.bfloat16
        )
        split_z = along_z.reshape(band_items, slab_planes, NG, 2, kept_count)
        along_y = jnp.einsum(
            "bxycz,cydk->bkxdz", split_z, forward_axis, preferred_element_type=jnp.float32
        )
        along_y = along_y.astype(jnp.bfloat16).reshape(
            band_items, kept_count, slab_planes, 2 * kept_count
        )
        exchanged = lax.all_to_all(along_y, "grid", split_axis=1, concat_axis=2, tiled=True)
        item_count = exchanged.shape[0]
        spread = exchanged.reshape(item_count, column_rows, NG, 2, kept_count)
        spectral = jnp.einsum(
            "byxcz,cxdk->bykdz", spread, forward_axis, preferred_element_type=jnp.float32
        )
        damped = (spectral * kinetic[None, :, :, None, :]).astype(jnp.bfloat16)
        spatial = jnp.einsum(
            "bykdz,dkcx->byxcz", damped, inverse_axis, preferred_element_type=jnp.float32
        )
        returned = lax.all_to_all(
            spatial.astype(jnp.bfloat16).reshape(item_count, column_rows, NG, 2 * kept_count),
            "grid",
            split_axis=2,
            concat_axis=1,
            tiled=True,
        )
        split_back = returned.reshape(band_items, kept_count, slab_planes, 2, kept_count)
        back_y = jnp.einsum(
            "bkxdz,dkcy->bxycz", split_back, inverse_axis, preferred_element_type=jnp.float32
        )
        back_y = back_y.astype(jnp.bfloat16).reshape(band_items, slab_planes, NG, 2 * kept_count)
        orbitals = jnp.dot(back_y, inverse_block, preferred_element_type=jnp.float32).astype(
            jnp.bfloat16
        )
        real_part = orbitals[..., :NG].astype(jnp.float32)
        imag_part = orbitals[..., NG:].astype(jnp.float32)
        weighted_sq = occupations[:, None, None, None] * (
            real_part * real_part + imag_part * imag_part
        )
        density_out = lax.psum(
            (jnp.sum(weighted_sq, axis=0) * (density_scale / bands_total)).astype(jnp.bfloat16),
            "band",
        )
        residual, newest, partial = residual_sums(
            iteration, hist_residual, fresh, density_out, density_now, residual_prev
        )
        fresh = fresh + [newest]
        density_diffs = density_diffs[-(DEPTH - 1) :] + [density_now - density_prev]
        residual_diffs = residual_diffs[-(DEPTH - 1) :] + [newest]
        sums = lax.psum(jnp.sum(partial, axis=(1, 2)) / cells_total, "grid")
        coeffs, gram_kept = solve_definite(gram_kept, sums, NG)
        density_next = density_now + mixing_weight * residual
        for j in range(DEPTH):
            combined = density_diffs[j] + mixing_weight * residual_diffs[j]
            density_next = density_next - coeffs[j][None, None, :] * combined
        density_prev = density_now
        residual_prev = residual
        density_now = density_next
    return (density_now, residual)


def solution(mesh):
    placed = (
        P(None, "band", "grid", None, None),
        P("band"),
        P("grid", None, None),
        P("grid", None, None),
        P("grid", None, None),
        P("grid", None, None),
        P(None, "grid", None, None),
        P(None, "grid", None, None),
    )
    return jax.shard_map(
        local,
        mesh=mesh,
        in_specs=placed,
        out_specs=(P("grid", None, None), P("grid", None, None)),
        check_vma=False,
    )
```
